32 devices in a mesh: ctx: 16 (over z, y, x), fsdp: 2 (over core).
Axes of the slice: x: 2, y: 2, z: 4, core: 2. Of those that a mesh axis runs over, the one named last changes fastest.
Arguments:
- block_input: bfloat16 [4, 1024, 1024], P('fsdp', 'ctx'), may hold values from -6 to 6
- cotangent: bfloat16 [4, 1024, 1024], P('fsdp', 'ctx'), may hold values from -6 to 6
- block_table: int32 [16, 2], replicated, may hold values from 0 to 31, as said below
- segments: int32 [4, 1024], P('fsdp'), may hold values from 0 to 2, as said below
- gain_one: bfloat16 [1024], P('fsdp'), may hold values from 0.25 to 1.75
- shift_one: bfloat16 [1024], P('fsdp'), may hold values from -3 to 3
- w_mix: bfloat16 [1024, 3072], P('fsdp'), may hold values from -0.1875 to 0.1875
- bias_query: bfloat16 [1024], P('fsdp'), may hold values from -3 to 3
- bias_value: bfloat16 [1024], P('fsdp'), may hold values from -3 to 3
- w_merge: bfloat16 [1024, 1024], P('fsdp'), may hold values from -0.375 to 0.375
- bias_merge: bfloat16 [1024], P('fsdp'), may hold values from -3 to 3
- gain_two: bfloat16 [1024], P('fsdp'), may hold values from 0.25 to 1.75
- shift_two: bfloat16 [1024], P('fsdp'), may hold values from -3 to 3
- w_expand: bfloat16 [1024, 4096], P('fsdp'), may hold values from -0.1875 to 0.1875
- bias_expand: bfloat16 [4096], P('fsdp'), may hold values from -3 to 3
- w_reduce: bfloat16 [4096, 1024], P('fsdp'), may hold values from -0.09375 to 0.09375
- bias_reduce: bfloat16 [1024], P('fsdp'), may hold values from -3 to 3
Outputs:
- block_output: bfloat16 [4, 1024, 1024], P('fsdp', 'ctx')
- grad_input: float32 [4, 1024, 1024], P('fsdp', 'ctx')
- grad_gain_one: float32 [1024], P(('ctx', 'fsdp'))
- grad_shift_one: float32 [1024], P(('ctx', 'fsdp'))
- grad_w_mix: float32 [1024, 3072], P(('ctx', 'fsdp'))
- grad_bias_query: float32 [1024], P(('ctx', 'fsdp'))
- grad_bias_value: float32 [1024], P(('ctx', 'fsdp'))
- grad_w_merge: float32 [1024, 1024], P(('ctx', 'fsdp'))
- grad_bias_merge: float32 [1024], P(('ctx', 'fsdp'))
- grad_gain_two: float32 [1024], P(('ctx', 'fsdp'))
- grad_shift_two: float32 [1024], P(('ctx', 'fsdp'))
- grad_w_expand: float32 [1024, 4096], P(('ctx', 'fsdp'))
- grad_bias_expand: float32 [4096], P(('ctx', 'fsdp'))
- grad_w_reduce: float32 [4096, 1024], P(('ctx', 'fsdp'))
- grad_bias_reduce: float32 [1024], P(('ctx', 'fsdp'))
The draws below stay inside these ranges and needn't reach their ends.
Inputs may be any that keep to these rules, and one draw needn't show every extreme that they name: `block_table`: row c lists the two blocks of 32 positions that the slots of index c of ctx hold, in slot order: a block b below 16, then its mirror 2 * 16 - 1 - b; every block appears once. `segments`: document ids by slot. Taken in order of position (slot s holds position block_table[s // 64, (s // 32) % 2] * 32 + s % 32), the ids of a sequence never fall, and each of its 3 documents holds at least one position.
All inputs are finite; a program needn't handle non-finite values.
Results may differ from the reference program's by a relative error of at most 0.02.
Values may be sent and summed in bfloat16 or wider, within the bound.
A program may use at most 320 MiB of HBM per device.

```python
import math
import jax
import jax.numpy as jnp
from jax import lax

D = 1024
HEADS = 16
FF = 4096
BLK = 32
SEGS = 3
LEN = 1024
SEQS = 4


def mirrored_blocks(key):
    ctx_count = LEN // (2 * BLK)
    lower = jax.random.permutation(jax.random.fold_in(key, 11), ctx_count).astype(jnp.int32)
    return jnp.stack([lower, 2 * ctx_count - 1 - lower], axis=1)


def draw_block_table(key, part):
    return mirrored_blocks(key)


def draw_segments(key, part):
    blocks = mirrored_blocks(key).reshape(-1)
    slot = jnp.arange(LEN, dtype=jnp.int32)
    position = blocks[slot // BLK] * BLK + slot % BLK
    reach = LEN // (4 * SEGS)
    jitter = jax.random.randint(jax.random.fold_in(key, 23), (SEQS, SEGS - 1), -reach, reach + 1, dtype=jnp.int32)
    cuts = jnp.arange(1, SEGS, dtype=jnp.int32) * LEN // SEGS + jitter
    return jnp.sum((position[None, :, None] >= cuts[:, None, :]).astype(jnp.int32), axis=2).astype(jnp.int32)


def with_spikes(array, own_key, source, target, parts, factor):
    owner, partner = [(jnp.arange(array.shape[axis_at]) // (array.shape[axis_at] // parts)).reshape([-1 if axis == axis_at else 1 for axis in range(array.ndim)]) for axis_at in (source, target)]
    chosen = jax.random.permutation(own_key, parts)[partner]
    strong = (owner == chosen) | (owner == (partner + parts // 2) % parts)
    return jnp.where(strong, factor * array, array)


def levels(key, shape, pieces, least, largest):
    def one(axis_at, shards_of):
        steps = jax.random.uniform(jax.random.fold_in(jax.random.fold_in(key, 6), axis_at), (shards_of,), jnp.float32, least / len(pieces), largest / len(pieces))
        return jnp.repeat(jnp.exp(steps), shape[axis_at] // shards_of).reshape((-1,) + (1,) * (len(shape) - axis_at - 1))

    level = one(*pieces[0])
    for cut in pieces[1:]:
        level = level * one(*cut)
    return level


def bell_draw(rng, shape, width, most, cuts=(), kind=jnp.bfloat16):
    entries = jax.random.normal(rng, shape, jnp.float32) * width
    if len(cuts) > 0:
        entries = levels(rng, shape, cuts, -0.22, 0.18) * entries
    return jnp.clip(entries, min=-most, max=most).astype(kind)


def heavy_noise(stream_key, extent, width, bound, split, heavy, kind=jnp.bfloat16):
    entries = width * jax.random.normal(stream_key, extent, jnp.float32)
    if split:
        entries = entries * levels(stream_key, extent, split, -0.22, 0.18)
    return jnp.clip(with_spikes(entries, jax.random.fold_in(stream_key, 3), *heavy), -bound, bound).astype(kind)


def setup_inputs(seed: int = 0) -> dict:
    splits = jax.random.split(jax.random.key(seed), 18)
    return {
        "block_input": bell_draw(splits[0], (SEQS, LEN, D), 1.0, 6.0, ((0, 2), (1, 16))),
        "cotangent": heavy_noise(splits[1], (SEQS, LEN, D), 1.0, 6.0, ((0, 2), (1, 16)), (1, 2, 16, 2.0)),
        "block_table": draw_block_table(jax.random.fold_in(splits[17], 71), 0),
        "segments": draw_segments(jax.random.fold_in(splits[17], 71), 0),
        "gain_one": jnp.clip(1.0 + 0.15 * jax.random.normal(splits[4], (D,), jnp.float32), 0.25, 1.75).astype(jnp.bfloat16),
        "shift_one": bell_draw(splits[5], (D,), 0.5, 3.0, ((0, 2),)),
        "w_mix": bell_draw(splits[6], (D, 3 * D), D ** -0.5, 0.1875, ((0, 2),)),
        "bias_query": bell_draw(splits[7], (D,), 0.5, 3.0, ((0, 2),)),
        "bias_value": bell_draw(splits[8], (D,), 0.5, 3.0, ((0, 2),)),
        "w_merge": bell_draw(splits[9], (D, D), (D // 4) ** -0.5, 0.375, ((0, 2),)),
        "bias_merge": bell_draw(splits[10], (D,), 0.5, 3.0, ((0, 2),)),
        "gain_two": jnp.clip(1.0 + 0.15 * jax.random.normal(splits[11], (D,), jnp.float32), 0.25, 1.75).astype(jnp.bfloat16),
        "shift_two": bell_draw(splits[12], (D,), 0.5, 3.0, ((0, 2),)),
        "w_expand": bell_draw(splits[13], (D, FF), D ** -0.5, 0.1875, ((0, 2),)),
        "bias_expand": bell_draw(splits[14], (FF,), 0.5, 3.0, ((0, 2),)),
        "w_reduce": bell_draw(splits[15], (FF, D), FF ** -0.5, 0.09375, ((0, 2),)),
        "bias_reduce": bell_draw(splits[16], (D,), 0.5, 3.0, ((0, 2),)),
    }


EPSILON = 1e-05
CUBIC = 0.044715
ROOT = math.sqrt(2.0 / math.pi)

def gelu_value(pre):
    inner = ROOT * (pre + CUBIC * pre * pre * pre)
    return 0.5 * pre * (1.0 + jnp.tanh(inner))

def gelu_slope(pre):
    inner = ROOT * (pre + CUBIC * pre * pre * pre)
    tangent = jnp.tanh(inner)
    return 0.5 * (1.0 + tangent) + 0.5 * pre * (1.0 - tangent * tangent) * ROOT * (1.0 + 3.0 * CUBIC * pre * pre)

def norm_forward(rows, gain, shift):
    center = rows - lax.optimization_barrier(jnp.mean(rows, axis=-1, keepdims=True))
    inverse = lax.rsqrt(lax.optimization_barrier(jnp.mean(center * center, axis=-1, keepdims=True)) + EPSILON)
    normed = center * inverse
    return (normed, inverse, (normed * gain.astype(jnp.float32) + shift.astype(jnp.float32)).astype(jnp.bfloat16))

def norm_backward(grad, normed, inverse, gain):
    scaled = grad * gain.astype(jnp.float32)
    return inverse * (scaled - lax.optimization_barrier(jnp.mean(scaled, axis=-1, keepdims=True)) - normed * lax.optimization_barrier(jnp.mean(scaled * normed, axis=-1, keepdims=True)))

def slot_positions(block_table, block):
    blocks = block_table.reshape(-1).astype(jnp.int32)
    return (blocks[:, None] * block + jnp.arange(block, dtype=jnp.int32)[None, :]).reshape(-1)

def widened(values):
    return lax.optimization_barrier(values).astype(jnp.float32)

def reference(block_input, cotangent, block_table, segments, gain_one, shift_one, w_mix, bias_query, bias_value, w_merge, bias_merge, gain_two, shift_two, w_expand, bias_expand, w_reduce, bias_reduce):
    length = block_input.shape[1]
    model = block_input.shape[2]
    block = length // (2 * block_table.shape[0])
    heads = HEADS
    head = model // heads
    scale = 1.0 / math.sqrt(head)
    position = slot_positions(block_table, block)
    offsets = jnp.concatenate([bias_query, jnp.zeros_like(bias_query), bias_value]).astype(jnp.float32)

    def one_sequence(carry, inputs):
        rows, upstream, segment = inputs
        visible = jnp.logical_and(position[None, :] <= position[:, None], segment[None, :] == segment[:, None])[None]
        tokens = rows.astype(jnp.float32)
        normed_one, inverse_one, first_in = norm_forward(tokens, gain_one, shift_one)
        mixed = lax.optimization_barrier((jnp.dot(first_in, w_mix, preferred_element_type=jnp.float32) + offsets).astype(jnp.bfloat16))
        wide = mixed.astype(jnp.float32)
        queries = wide[:, :model].reshape(length, heads, head)
        keys = wide[:, model:2 * model].reshape(length, heads, head)
        values = wide[:, 2 * model:].reshape(length, heads, head)
        scores = jnp.einsum('shd,thd->hst', queries, keys) * scale
        expo = jnp.where(visible, jnp.exp(scores), 0.0)
        total = lax.optimization_barrier(jnp.sum(expo, axis=-1))
        summed = jnp.einsum('hst,thd->shd', widened(expo.astype(jnp.bfloat16)), values)
        context = lax.optimization_barrier((summed / total.T[:, :, None]).reshape(length, model).astype(jnp.bfloat16))
        log_total = jnp.log(total)
        resid = tokens + jnp.dot(context, w_merge, preferred_element_type=jnp.float32) + bias_merge.astype(jnp.float32)
        normed_two, inverse_two, second_in = norm_forward(resid, gain_two, shift_two)
        pre = jnp.dot(second_in, w_expand, preferred_element_type=jnp.float32) + bias_expand.astype(jnp.float32)
        act = gelu_value(pre).astype(jnp.bfloat16)
        output = (resid + jnp.dot(act, w_reduce, preferred_element_type=jnp.float32) + bias_reduce.astype(jnp.float32)).astype(jnp.bfloat16)
        incoming = upstream.astype(jnp.float32)
        grad_reduce = jnp.dot(act.T, upstream, preferred_element_type=jnp.float32)
        grad_pre = jnp.dot(upstream, w_reduce.T, preferred_element_type=jnp.float32) * gelu_slope(pre)
        pre_rounded = grad_pre.astype(jnp.bfloat16)
        grad_expand = jnp.dot(second_in.T, pre_rounded, preferred_element_type=jnp.float32)
        grad_second = jnp.dot(pre_rounded, w_expand.T, preferred_element_type=jnp.float32)
        grad_resid = incoming + norm_backward(grad_second, normed_two, inverse_two, gain_two)
        resid_rounded = grad_resid.astype(jnp.bfloat16)
        grad_merge = jnp.dot(context.T, resid_rounded, preferred_element_type=jnp.float32)
        grad_context = lax.optimization_barrier(jnp.dot(resid_rounded, w_merge.T, preferred_element_type=jnp.float32).astype(jnp.bfloat16))
        grad_wide = grad_context.astype(jnp.float32)
        delta = lax.optimization_barrier(jnp.sum((grad_wide * context.astype(jnp.float32)).reshape(length, heads, head), axis=-1)).T
        grad_heads = grad_wide.reshape(length, heads, head)
        prob = jnp.where(visible, jnp.exp(scores - log_total[:, :, None]), 0.0)
        dprob = jnp.einsum('shd,thd->hst', grad_heads, values)
        grad_score = prob * (dprob - delta[:, :, None])
        score_rounded = widened(grad_score.astype(jnp.bfloat16))
        grad_query = jnp.einsum('hst,thd->shd', score_rounded, keys).reshape(length, model) * scale
        grad_key = jnp.einsum('hst,shd->thd', score_rounded, queries).reshape(length, model) * scale
        grad_value = jnp.einsum('hst,shd->thd', widened(prob.astype(jnp.bfloat16)), grad_heads).reshape(length, model)
        grad_mixed = jnp.concatenate([grad_query, grad_key, grad_value], axis=1).astype(jnp.bfloat16)
        grad_mix = jnp.dot(first_in.T, grad_mixed, preferred_element_type=jnp.float32)
        grad_first = jnp.dot(grad_mixed, w_mix.T, preferred_element_type=jnp.float32)
        grad_in = grad_resid + norm_backward(grad_first, normed_one, inverse_one, gain_one)
        terms = (lax.optimization_barrier(jnp.sum(grad_first * normed_one, axis=0)), lax.optimization_barrier(jnp.sum(grad_first, axis=0)), grad_mix, lax.optimization_barrier(jnp.sum(grad_query, axis=0)), lax.optimization_barrier(jnp.sum(grad_value, axis=0)), grad_merge, lax.optimization_barrier(jnp.sum(grad_resid, axis=0)), lax.optimization_barrier(jnp.sum(grad_second * normed_two, axis=0)), lax.optimization_barrier(jnp.sum(grad_second, axis=0)), grad_expand, lax.optimization_barrier(jnp.sum(grad_pre, axis=0)), grad_reduce, lax.optimization_barrier(jnp.sum(incoming, axis=0)))
        updated = tuple((older + newer for older, newer in zip(carry, terms)))
        return (updated, (output, grad_in))
    hidden = w_expand.shape[1]
    shapes = [(model,), (model,), (model, 3 * model), (model,), (model,), (model, model), (model,), (model,), (model,), (model, hidden), (hidden,), (hidden, model), (model,)]
    start = tuple((jnp.zeros(shape, jnp.float32) for shape in shapes))
    sums, emitted = lax.scan(one_sequence, start, (block_input, cotangent, segments))
    return (emitted[0], emitted[1], sums[0], sums[1], sums[2], sums[3], sums[4], sums[5], sums[6], sums[7], sums[8], sums[9], sums[10], sums[11], sums[12])
```

```python
import functools
import math

import jax
import jax.numpy as jnp
from jax import lax
from jax.sharding import PartitionSpec as P

HEADS = 16


EPSILON = 1e-05
CUBIC = 0.044715
ROOT = math.sqrt(2.0 / math.pi)


def gelu_value(pre):
    inner = ROOT * (pre + CUBIC * pre * pre * pre)
    return 0.5 * pre * (1.0 + jnp.tanh(inner))


def gelu_slope(pre):
    inner = ROOT * (pre + CUBIC * pre * pre * pre)
    tangent = jnp.tanh(inner)
    return 0.5 * (1.0 + tangent) + 0.5 * pre * (1.0 - tangent * tangent) * ROOT * (
        1.0 + 3.0 * CUBIC * pre * pre
    )


def norm_forward(rows, gain, shift):
    center = rows - jnp.mean(rows, axis=-1, keepdims=True)
    inverse = lax.rsqrt(jnp.mean(center * center, axis=-1, keepdims=True) + EPSILON)
    normed = center * inverse
    return (
        normed,
        inverse,
        (normed * gain.astype(jnp.float32) + shift.astype(jnp.float32)).astype(jnp.bfloat16),
    )


def norm_backward(grad, normed, inverse, gain):
    scaled = grad * gain.astype(jnp.float32)
    return inverse * (
        scaled
        - jnp.mean(scaled, axis=-1, keepdims=True)
        - normed * jnp.mean(scaled * normed, axis=-1, keepdims=True)
    )


def slot_positions(block_table, block):
    blocks = block_table.reshape(-1)
    return (blocks[:, None] * block + jnp.arange(block, dtype=jnp.int32)[None, :]).reshape(-1)


def halving_bits(count):
    return count.bit_length() - 1


def partner_pairs(count, bit):
    return [(i, i ^ (1 << bit)) for i in range(count)]


def fsdp_halves(rows, n_ctx, n_fsdp, mine):
    tokens, columns = rows.shape
    parts = rows.reshape(tokens, n_ctx, n_fsdp, columns // (n_ctx * n_fsdp))
    kept = lax.dynamic_index_in_dim(parts, mine, 2, keepdims=False)
    sent = lax.dynamic_index_in_dim(parts, 1 - mine, 2, keepdims=False)
    return sent.reshape(tokens, -1), kept.reshape(tokens, -1)


def scatter_bits(block, n_ctx, order):
    bits = halving_bits(n_ctx)
    index = lax.axis_index("ctx")
    held = list(reversed(range(bits)))
    block = block.reshape((2,) * bits + block.shape[1:])
    kind = block.dtype
    for step, bit in enumerate(order):
        at = held.index(bit)
        own = lax.rem(lax.div(index, 1 << bit), 2)
        sent = lax.dynamic_index_in_dim(block, 1 - own, at, keepdims=False)
        kept = lax.dynamic_index_in_dim(block, own, at, keepdims=False)
        came = lax.ppermute(sent, "ctx", partner_pairs(n_ctx, bit))
        block = kept.astype(jnp.float32) + came.astype(jnp.float32)
        if step < bits - 1:
            block = block.astype(kind)
        held.remove(bit)
    return block


def weight_grad(left, right, order, n_ctx, n_fsdp):
    if n_fsdp != 2 or n_ctx != 1 << halving_bits(n_ctx):
        full = jnp.einsum("ti,tj->ij", left, right, preferred_element_type=jnp.float32)
        return lax.psum_scatter(full, ("ctx", "fsdp"), scatter_dimension=0, tiled=True)
    sent, kept = fsdp_halves(left, n_ctx, n_fsdp, lax.axis_index("fsdp"))
    away = jnp.einsum("ti,tj->ij", sent, right, preferred_element_type=jnp.float32)
    came = lax.ppermute(away.astype(jnp.bfloat16), "fsdp", [(0, 1), (1, 0)])
    here = jnp.einsum("ti,tj->ij", kept, right, preferred_element_type=jnp.float32)
    block = (here + came.astype(jnp.float32)).astype(jnp.bfloat16)
    block = block.reshape(n_ctx, -1, right.shape[1])
    return scatter_bits(block, n_ctx, order)


def vector_grads(vectors, n_ctx, n_fsdp):
    count = n_ctx * n_fsdp
    widths = [v.shape[0] // count for v in vectors]
    packed = jnp.concatenate([v.reshape(count, -1) for v in vectors], axis=1)
    if n_fsdp != 2 or n_ctx != 1 << halving_bits(n_ctx):
        own = lax.psum_scatter(packed, ("ctx", "fsdp"), scatter_dimension=0, tiled=True)
    else:
        parts = packed.reshape(n_ctx, n_fsdp, -1)
        mine = lax.axis_index("fsdp")
        sent = lax.dynamic_index_in_dim(parts, 1 - mine, 1, keepdims=False)
        kept = lax.dynamic_index_in_dim(parts, mine, 1, keepdims=False)
        kept = kept + lax.ppermute(sent, "fsdp", [(0, 1), (1, 0)])
        own = scatter_bits(kept, n_ctx, list(range(halving_bits(n_ctx))))
    own = own.reshape(-1)
    outs, at = [], 0
    for width in widths:
        outs.append(own[at : at + width])
        at += width
    return outs


def to_heads(rows, groups, pieces, n_ctx):
    width = rows.shape[0] // groups
    part = rows.shape[1] // (pieces * n_ctx)
    blocks = rows.reshape(groups, width, pieces, n_ctx, part).transpose(3, 2, 1, 0, 4)
    blocks = blocks.reshape(n_ctx, pieces, width, groups * part)
    blocks = lax.all_to_all(blocks, "ctx", 0, 0, tiled=True)
    blocks = blocks.transpose(1, 0, 2, 3)
    return blocks.reshape(pieces, n_ctx * width, groups, part)


def to_tokens(blocks, n_ctx):
    pieces, length, groups, part = blocks.shape
    width = length // n_ctx
    blocks = blocks.reshape(pieces, n_ctx, width, groups * part).transpose(1, 0, 2, 3)
    blocks = lax.all_to_all(blocks, "ctx", 0, 0, tiled=True)
    blocks = blocks.reshape(n_ctx, pieces, width, groups, part).transpose(3, 2, 1, 0, 4)
    return blocks.reshape(groups * width, pieces * n_ctx * part)


def body(
    n_ctx,
    n_fsdp,
    block_input,
    cotangent,
    block_table,
    segments,
    gain_one,
    shift_one,
    w_mix,
    bias_query,
    bias_value,
    w_merge,
    bias_merge,
    gain_two,
    shift_two,
    w_expand,
    bias_expand,
    w_reduce,
    bias_reduce,
):
    groups, width, model = block_input.shape
    length = segments.shape[1]
    heads = HEADS
    head = model // heads
    half_heads = heads // 2
    scale = 1.0 / math.sqrt(head)
    (
        gain_one,
        shift_one,
        w_mix,
        bias_query,
        bias_value,
        w_merge,
        bias_merge,
        gain_two,
        shift_two,
        w_expand,
        bias_expand,
        w_reduce,
        bias_reduce,
    ) = (
        lax.all_gather(gain_one, "fsdp", axis=0, tiled=True),
        lax.all_gather(shift_one, "fsdp", axis=0, tiled=True),
        lax.all_gather(w_mix, "fsdp", axis=0, tiled=True),
        lax.all_gather(bias_query, "fsdp", axis=0, tiled=True),
        lax.all_gather(bias_value, "fsdp", axis=0, tiled=True),
        lax.all_gather(w_merge, "fsdp", axis=0, tiled=True),
        lax.all_gather(bias_merge, "fsdp", axis=0, tiled=True),
        lax.all_gather(gain_two, "fsdp", axis=0, tiled=True),
        lax.all_gather(shift_two, "fsdp", axis=0, tiled=True),
        lax.all_gather(w_expand, "fsdp", axis=0, tiled=True),
        lax.all_gather(bias_expand, "fsdp", axis=0, tiled=True),
        lax.all_gather(w_reduce, "fsdp", axis=0, tiled=True),
        lax.all_gather(bias_reduce, "fsdp", axis=0, tiled=True),
    )
    key_position = slot_positions(block_table, width // 2)
    by_heads = heads % n_ctx == 0
    if by_heads:
        visible = jnp.logical_and(
            key_position[None, None, :] <= key_position[None, :, None],
            segments[:, None, :] == segments[:, :, None],
        )
    else:
        first_slot = lax.axis_index("ctx") * width
        query_position = lax.dynamic_slice_in_dim(key_position, first_slot, width)
        query_segment = lax.dynamic_slice_in_dim(segments, first_slot, width, axis=1)
        visible = jnp.logical_and(
            key_position[None, None, :] <= query_position[None, :, None],
            segments[:, None, :] == query_segment[:, :, None],
        )
    tokens = block_input.reshape(groups * width, model).astype(jnp.float32)
    normed_one, inverse_one, first_in = norm_forward(tokens, gain_one, shift_one)
    offsets = jnp.concatenate([bias_query, jnp.zeros_like(bias_query), bias_value]).astype(
        jnp.float32
    )
    mixed = (jnp.dot(first_in, w_mix, preferred_element_type=jnp.float32) + offsets).astype(
        jnp.bfloat16
    )
    if by_heads:
        own = heads // n_ctx
        queries, keys, values = to_heads(mixed, groups, 3, n_ctx).reshape(
            3, length, groups, own, head
        )
        scores = (
            jnp.einsum("sghd,tghd->ghst", queries, keys, preferred_element_type=jnp.float32)
            * scale
        )
        expo = jnp.where(visible[:, None], jnp.exp(scores), 0.0)
        total = jnp.sum(expo, axis=-1)
        summed = jnp.einsum(
            "ghst,tghd->sghd",
            expo.astype(jnp.bfloat16),
            values,
            preferred_element_type=jnp.float32,
        )
        context = (summed / total.transpose(2, 0, 1)[..., None]).astype(jnp.bfloat16)
        log_total = jnp.log(total)
        context_rows = to_tokens(context.reshape(1, length, groups, own * head), n_ctx)
    else:
        queries = mixed[:, :model].reshape(groups, width, heads, head)
        local_pairs = mixed[:, model:].reshape(groups, width, 2 * model)
        pairs = lax.all_gather(local_pairs, "ctx", axis=1, tiled=True)
        keys = pairs[:, :, :model].reshape(groups, length, heads, head)
        values = pairs[:, :, model:].reshape(groups, length, heads, head)
        context_parts, log_parts = ([], [])
        for half in range(2):
            first = half * half_heads
            part_scores = (
                jnp.einsum(
                    "gshd,gthd->ghst",
                    queries[:, :, first : first + half_heads],
                    keys[:, :, first : first + half_heads],
                    preferred_element_type=jnp.float32,
                )
                * scale
            )
            expo = jnp.where(visible[:, None], jnp.exp(part_scores), 0.0)
            total = jnp.sum(expo, axis=-1)
            summed = jnp.einsum(
                "ghst,gthd->gshd",
                expo.astype(jnp.bfloat16),
                values[:, :, first : first + half_heads],
                preferred_element_type=jnp.float32,
            )
            context_parts.append(summed / jnp.swapaxes(total, 1, 2)[..., None])
            log_parts.append(jnp.log(total))
        context = jnp.concatenate(context_parts, axis=2).astype(jnp.bfloat16)
        log_total = jnp.concatenate(log_parts, axis=1)
        context_rows = context.reshape(groups * width, model)
    resid = (
        tokens
        + jnp.dot(context_rows, w_merge, preferred_element_type=jnp.float32)
        + bias_merge.astype(jnp.float32)
    )
    normed_two, inverse_two, second_in = norm_forward(resid, gain_two, shift_two)
    pre = jnp.dot(second_in, w_expand, preferred_element_type=jnp.float32) + bias_expand.astype(
        jnp.float32
    )
    act = gelu_value(pre).astype(jnp.bfloat16)
    block_output = (
        resid
        + jnp.dot(act, w_reduce, preferred_element_type=jnp.float32)
        + bias_reduce.astype(jnp.float32)
    ).astype(jnp.bfloat16)
    upstream = cotangent.reshape(groups * width, model)
    incoming = upstream.astype(jnp.float32)
    grad_pre = jnp.einsum(
        "tj,ij->ti", upstream, w_reduce, preferred_element_type=jnp.float32
    ) * gelu_slope(pre)
    pre_rounded = grad_pre.astype(jnp.bfloat16)
    bits = list(range(halving_bits(n_ctx)))
    swapped = bits[1::-1] + bits[2:]
    grad_reduce = weight_grad(act, upstream, bits, n_ctx, n_fsdp)
    grad_expand = weight_grad(second_in, pre_rounded, swapped, n_ctx, n_fsdp)
    grad_second = jnp.einsum("tj,ij->ti", pre_rounded, w_expand, preferred_element_type=jnp.float32)
    grad_resid = incoming + norm_backward(grad_second, normed_two, inverse_two, gain_two)
    resid_rounded = grad_resid.astype(jnp.bfloat16)
    grad_merge = weight_grad(context_rows, resid_rounded, bits, n_ctx, n_fsdp)
    grad_context = jnp.einsum(
        "tj,ij->ti", resid_rounded, w_merge, preferred_element_type=jnp.float32
    ).astype(jnp.bfloat16)
    if by_heads:
        grad_heads = to_heads(grad_context, groups, 1, n_ctx).reshape(length, groups, own, head)
        delta = jnp.sum(grad_heads.astype(jnp.float32) * context.astype(jnp.float32), axis=-1)
        scores = (
            jnp.einsum("sghd,tghd->ghst", queries, keys, preferred_element_type=jnp.float32)
            * scale
        )
        prob = jnp.where(visible[:, None], jnp.exp(scores - log_total[..., None]), 0.0)
        dprob = jnp.einsum(
            "sghd,tghd->ghst", grad_heads, values, preferred_element_type=jnp.float32
        )
        score_rounded = (prob * (dprob - delta.transpose(1, 2, 0)[..., None])).astype(
            jnp.bfloat16
        )
        grad_query = (
            jnp.einsum("ghst,tghd->sghd", score_rounded, keys, preferred_element_type=jnp.float32)
            * scale
        )
        grad_key = (
            jnp.einsum(
                "ghst,sghd->tghd", score_rounded, queries, preferred_element_type=jnp.float32
            )
            * scale
        )
        grad_value = jnp.einsum(
            "ghst,sghd->tghd",
            prob.astype(jnp.bfloat16),
            grad_heads,
            preferred_element_type=jnp.float32,
        )
        bias_sums = jnp.stack(
            [
                jnp.sum(grad_query, axis=(0, 1)).reshape(-1),
                jnp.sum(grad_value, axis=(0, 1)).reshape(-1),
            ]
        )
        placed = jnp.zeros((2, n_ctx, own * head), jnp.float32)
        placed = lax.dynamic_update_slice_in_dim(
            placed, bias_sums[:, None], lax.axis_index("ctx"), 1
        )
        query_sum, value_sum = placed.reshape(2, model)
        grad_mixed = to_tokens(
            jnp.stack([grad_query, grad_key, grad_value])
            .astype(jnp.bfloat16)
            .reshape(3, length, groups, own * head),
            n_ctx,
        )
    else:
        delta = jnp.sum(
            (grad_context.astype(jnp.float32) * context_rows.astype(jnp.float32)).reshape(
                groups, width, heads, head
            ),
            axis=-1,
        )
        delta = jnp.swapaxes(delta, 1, 2)
        grad_heads = grad_context.reshape(groups, width, heads, head)
        query_parts, key_parts, value_parts = ([], [], [])
        for half in range(2):
            first = half * half_heads
            query_part = queries[:, :, first : first + half_heads]
            key_part = keys[:, :, first : first + half_heads]
            value_part = values[:, :, first : first + half_heads]
            grad_part = grad_heads[:, :, first : first + half_heads]
            part_scores = (
                jnp.einsum("gshd,gthd->ghst", query_part, key_part, preferred_element_type=jnp.float32)
                * scale
            )
            prob = jnp.where(
                visible[:, None],
                jnp.exp(part_scores - log_total[:, first : first + half_heads, :, None]),
                0.0,
            )
            dprob = jnp.einsum(
                "gshd,gthd->ghst", grad_part, value_part, preferred_element_type=jnp.float32
            )
            grad_score = prob * (dprob - delta[:, first : first + half_heads, :, None])
            score_rounded = grad_score.astype(jnp.bfloat16)
            query_parts.append(
                jnp.einsum(
                    "ghst,gthd->gshd", score_rounded, key_part, preferred_element_type=jnp.float32
                )
                * scale
            )
            key_term = (
                jnp.einsum(
                    "ghst,gshd->gthd", score_rounded, query_part, preferred_element_type=jnp.float32
                )
                * scale
            )
            value_term = jnp.einsum(
                "ghst,gshd->gthd",
                prob.astype(jnp.bfloat16),
                grad_part,
                preferred_element_type=jnp.float32,
            )
            key_sum, value_sum = (
                lax.psum_scatter(
                    key_term.reshape(groups, length, half_heads * head),
                    "ctx",
                    scatter_dimension=1,
                    tiled=True,
                ),
                lax.psum_scatter(
                    value_term.reshape(groups, length, half_heads * head),
                    "ctx",
                    scatter_dimension=1,
                    tiled=True,
                ),
            )
            key_parts.append(key_sum)
            value_parts.append(value_sum)
        grad_query = jnp.concatenate(query_parts, axis=2)
        grad_key = jnp.concatenate(key_parts, axis=2)
        grad_value = jnp.concatenate(value_parts, axis=2)
        query_rows_grad = grad_query.reshape(groups * width, model)
        key_rows_grad = grad_key.reshape(groups * width, model)
        value_rows_grad = grad_value.reshape(groups * width, model)
        query_sum = jnp.sum(query_rows_grad, axis=0)
        value_sum = jnp.sum(value_rows_grad, axis=0)
        grad_mixed = jnp.concatenate(
            [query_rows_grad, key_rows_grad, value_rows_grad], axis=1
        ).astype(jnp.bfloat16)
    middle = grad_mixed.shape[1] // 2
    grad_mix = jnp.concatenate(
        [
            weight_grad(first_in, grad_mixed[:, :middle], bits, n_ctx, n_fsdp),
            weight_grad(first_in, grad_mixed[:, middle:], swapped, n_ctx, n_fsdp),
        ],
        axis=1,
    )
    grad_first = jnp.einsum("tj,ij->ti", grad_mixed, w_mix, preferred_element_type=jnp.float32)
    grad_tokens = grad_resid + norm_backward(grad_first, normed_one, inverse_one, gain_one)
    sums = vector_grads(
        [
            jnp.sum(grad_first * normed_one, axis=0),
            jnp.sum(grad_first, axis=0),
            query_sum,
            value_sum,
            jnp.sum(grad_resid, axis=0),
            jnp.sum(grad_second * normed_two, axis=0),
            jnp.sum(grad_second, axis=0),
            jnp.sum(grad_pre, axis=0),
            jnp.sum(incoming, axis=0),
        ],
        n_ctx,
        n_fsdp,
    )
    return (
        block_output.reshape(groups, width, model),
        grad_tokens.reshape(groups, width, model),
        sums[0],
        sums[1],
        grad_mix,
        sums[2],
        sums[3],
        grad_merge,
        sums[4],
        sums[5],
        sums[6],
        grad_expand,
        sums[7],
        grad_reduce,
        sums[8],
    )


def solution(mesh):
    in_specs = (
        P("fsdp", "ctx", None),
        P("fsdp", "ctx", None),
        P(),
        P("fsdp", None),
        P("fsdp"),
        P("fsdp"),
        P("fsdp", None),
        P("fsdp"),
        P("fsdp"),
        P("fsdp", None),
        P("fsdp"),
        P("fsdp"),
        P("fsdp"),
        P("fsdp", None),
        P("fsdp"),
        P("fsdp", None),
        P("fsdp"),
    )
    out_specs = (
        P("fsdp", "ctx", None),
        P("fsdp", "ctx", None),
        P(("ctx", "fsdp")),
        P(("ctx", "fsdp")),
        P(("ctx", "fsdp"), None),
        P(("ctx", "fsdp")),
        P(("ctx", "fsdp")),
        P(("ctx", "fsdp"), None),
        P(("ctx", "fsdp")),
        P(("ctx", "fsdp")),
        P(("ctx", "fsdp")),
        P(("ctx", "fsdp"), None),
        P(("ctx", "fsdp")),
        P(("ctx", "fsdp"), None),
        P(("ctx", "fsdp")),
    )
    return jax.shard_map(
        functools.partial(body, mesh.shape["ctx"], mesh.shape["fsdp"]),
        mesh=mesh,
        in_specs=in_specs, out_specs=out_specs, check_vma=False)
```

```python
import functools
import math

import jax
import jax.numpy as jnp
from jax import lax
from jax.experimental import pallas as pl
from jax.experimental.pallas import tpu as pltpu
from jax.sharding import PartitionSpec as P

HEADS = 16


EPSILON = 1e-05
CUBIC = 0.044715
ROOT = math.sqrt(2.0 / math.pi)


def gelu_value(pre):
    inner = ROOT * (pre + CUBIC * pre * pre * pre)
    return 0.5 * pre * (1.0 + jnp.tanh(inner))


def gelu_slope(pre):
    inner = ROOT * (pre + CUBIC * pre * pre * pre)
    tangent = jnp.tanh(inner)
    return 0.5 * (1.0 + tangent) + 0.5 * pre * (1.0 - tangent * tangent) * ROOT * (
        1.0 + 3.0 * CUBIC * pre * pre
    )


def norm_forward(rows, gain, shift):
    center = rows - jnp.mean(rows, axis=-1, keepdims=True)
    inverse = lax.rsqrt(jnp.mean(center * center, axis=-1, keepdims=True) + EPSILON)
    normed = center * inverse
    return (
        normed,
        inverse,
        (normed * gain.astype(jnp.float32) + shift.astype(jnp.float32)).astype(jnp.bfloat16),
    )


def norm_backward(grad, normed, inverse, gain):
    scaled = grad * gain.astype(jnp.float32)
    return inverse * (
        scaled
        - jnp.mean(scaled, axis=-1, keepdims=True)
        - normed * jnp.mean(scaled * normed, axis=-1, keepdims=True)
    )


def slot_positions(block_table, block):
    blocks = block_table.reshape(-1)
    return (blocks[:, None] * block + jnp.arange(block, dtype=jnp.int32)[None, :]).reshape(-1)


def halving_bits(count):
    return count.bit_length() - 1


def partner_pairs(count, bit):
    return [(i, i ^ (1 << bit)) for i in range(count)]


class Exchange:
    def __init__(self, sent, kept, kind, order, n_ctx):
        self.sent, self.kept, self.kind, self.n_ctx = sent, kept, kind, n_ctx
        self.order = list(order)
        self.held = list(reversed(range(halving_bits(n_ctx))))
        self.bit = None
        self.result = None

    def go(self):
        if self.sent is None:
            return
        if self.bit is None:
            came = lax.ppermute(self.sent, "fsdp", [(0, 1), (1, 0)])
        else:
            came = lax.ppermute(self.sent, "ctx", partner_pairs(self.n_ctx, self.bit))
        block = self.kept().astype(jnp.float32) + came.astype(jnp.float32)
        if not self.order:
            self.sent, self.result = None, block
            return
        block = block.astype(self.kind)
        if self.bit is None:
            block = block.reshape((2,) * len(self.held) + (-1, block.shape[-1]))
        self.bit = self.order.pop(0)
        at = self.held.index(self.bit)
        own = lax.rem(lax.div(lax.axis_index("ctx"), 1 << self.bit), 2)
        self.sent = lax.dynamic_index_in_dim(block, 1 - own, at, keepdims=False)
        self.kept = lambda: lax.dynamic_index_in_dim(block, own, at, keepdims=False)
        self.held.remove(self.bit)

    def finish(self):
        while self.sent is not None:
            self.go()
        return self.result


class Whole:
    def __init__(self, full):
        self.sent = None
        self.full = full

    def go(self):
        pass

    def finish(self):
        return lax.psum_scatter(self.full, ("ctx", "fsdp"), scatter_dimension=0, tiled=True)


def advance(anchor, *exchanges):
    live = [e for e in exchanges if e.sent is not None]
    anchor, *sent = lax.optimization_barrier((anchor, *[e.sent for e in live]))
    for e, value in zip(live, sent):
        e.sent = value
        e.go()
    return anchor


def weight_grad(left, right, order, n_ctx, n_fsdp):
    if n_fsdp != 2 or n_ctx != 1 << halving_bits(n_ctx):
        return Whole(jnp.einsum("ti,tj->ij", left, right, preferred_element_type=jnp.float32))
    full = jnp.einsum("ti,tj->ij", left, right, preferred_element_type=jnp.float32)
    full = full.astype(jnp.bfloat16).reshape(n_ctx, n_fsdp, -1, right.shape[1])
    mine = lax.axis_index("fsdp")
    return Exchange(
        lax.dynamic_index_in_dim(full, 1 - mine, 1, keepdims=False),
        lambda: lax.dynamic_index_in_dim(full, mine, 1, keepdims=False),
        jnp.bfloat16,
        order,
        n_ctx,
    )


def vector_grads(vectors, order, n_ctx, n_fsdp):
    count = n_ctx * n_fsdp
    packed = jnp.concatenate([v.reshape(count, -1) for v in vectors], axis=1)
    if n_fsdp != 2 or n_ctx != 1 << halving_bits(n_ctx):
        return Whole(packed)
    parts = packed.reshape(n_ctx, n_fsdp, -1)
    mine = lax.axis_index("fsdp")
    return Exchange(
        lax.dynamic_index_in_dim(parts, 1 - mine, 1, keepdims=False),
        lambda: lax.dynamic_index_in_dim(parts, mine, 1, keepdims=False),
        jnp.float32,
        order,
        n_ctx,
    )


def to_heads(rows, groups, pieces, n_ctx):
    width = rows.shape[0] // groups
    part = rows.shape[1] // (pieces * n_ctx)
    blocks = rows.reshape(groups, width, pieces, n_ctx, part).transpose(3, 2, 1, 0, 4)
    blocks = blocks.reshape(n_ctx, pieces, width, groups * part)
    return lax.all_to_all(blocks, "ctx", 0, 0, tiled=True)


def to_tokens(blocks, groups):
    blocks = lax.all_to_all(blocks, "ctx", 0, 0, tiled=True)
    n_ctx, pieces, width, lanes = blocks.shape
    part = lanes // groups
    blocks = blocks.reshape(n_ctx, pieces, width, groups, part).transpose(3, 2, 1, 0, 4)
    return blocks.reshape(groups * width, pieces * n_ctx * part)


def visible_tile(pos_col, seg_col, pos_row, seg_row, group):
    return jnp.logical_and(
        pos_row[...] <= pos_col[...],
        seg_row[group : group + 1, :] == seg_col[:, group : group + 1],
    )


def tile_scores(query, key, scale):
    return (
        lax.dot_general(
            query, key, (((1,), (1,)), ((), ())), preferred_element_type=jnp.float32
        )
        * scale
    )


def attend_kernel(units, own, head, scale, span, qkv, pos_col, seg_col, pos_row, seg_row, out):
    first = pl.program_id(0) * span
    sources, _, width, lanes = qkv.shape
    query = qkv[pl.ds(first, span), 0].reshape(span * width, lanes)
    key = qkv[:, 1].reshape(sources * width, lanes)
    value = qkv[:, 2].reshape(sources * width, lanes)
    parts = []
    for unit in range(units):
        at = slice(unit * head, (unit + 1) * head)
        seen = visible_tile(pos_col, seg_col, pos_row, seg_row, unit // own)
        expo = jnp.where(seen, jnp.exp(tile_scores(query[:, at], key[:, at], scale)), 0.0)
        total = jnp.sum(expo, axis=-1, keepdims=True)
        summed = jnp.dot(
            expo.astype(jnp.bfloat16), value[:, at], preferred_element_type=jnp.float32
        )
        parts.append(summed / total)
    out[...] = jnp.concatenate(parts, axis=1).astype(jnp.bfloat16).reshape(out.shape)


def attend_back_kernel(
    units, own, head, scale, span, qkv, context, grad, pos_col, seg_col, pos_row, seg_row,
    out, sums, key_sum, value_sum,
):
    tile = pl.program_id(0)
    first = tile * span
    sources, _, width, lanes = qkv.shape
    query = qkv[pl.ds(first, span), 0].reshape(span * width, lanes)
    key = qkv[:, 1].reshape(sources * width, lanes)
    value = qkv[:, 2].reshape(sources * width, lanes)
    upper = grad[...].reshape(span * width, lanes)
    product = upper.astype(jnp.float32) * context[...].reshape(span * width, lanes).astype(
        jnp.float32
    )

    @pl.when(tile == 0)
    def _():
        key_sum[...] = jnp.zeros_like(key_sum)
        value_sum[...] = jnp.zeros_like(value_sum)
        sums[...] = jnp.zeros_like(sums)

    parts = []
    for unit in range(units):
        at = slice(unit * head, (unit + 1) * head)
        seen = visible_tile(pos_col, seg_col, pos_row, seg_row, unit // own)
        scores = tile_scores(query[:, at], key[:, at], scale)
        total = jnp.sum(jnp.where(seen, jnp.exp(scores), 0.0), axis=-1, keepdims=True)
        prob = jnp.where(seen, jnp.exp(scores - jnp.log(total)), 0.0)
        dprob = lax.dot_general(
            upper[:, at], value[:, at], (((1,), (1,)), ((), ())), preferred_element_type=jnp.float32
        )
        delta = jnp.sum(product[:, at], axis=-1, keepdims=True)
        rounded = (prob * (dprob - delta)).astype(jnp.bfloat16)
        parts.append(jnp.dot(rounded, key[:, at], preferred_element_type=jnp.float32) * scale)
        key_sum[at, :] += lax.dot_general(
            query[:, at], rounded, (((0,), (0,)), ((), ())), preferred_element_type=jnp.float32
        )
        value_sum[at, :] += lax.dot_general(
            upper[:, at],
            prob.astype(jnp.bfloat16),
            (((0,), (0,)), ((), ())),
            preferred_element_type=jnp.float32,
        )
    grad_query = jnp.concatenate(parts, axis=1)
    sums[0:1, :] += jnp.sum(grad_query, axis=0, keepdims=True)
    out[pl.ds(first, span), 0] = grad_query.astype(jnp.bfloat16).reshape(span, width, lanes)

    @pl.when(tile == pl.num_programs(0) - 1)
    def _():
        grad_value = value_sum[...].T
        sums[1:2, :] = jnp.sum(grad_value, axis=0, keepdims=True)
        grad_key = (key_sum[...] * scale).T
        out[:, 1] = grad_key.astype(jnp.bfloat16).reshape(sources, width, lanes)
        out[:, 2] = grad_value.astype(jnp.bfloat16).reshape(sources, width, lanes)


def attention_call(kernel, extra, outs, scratch, own, head, qkv, position, segments):
    sources, pieces, width, lanes = qkv.shape
    groups, length = segments.shape
    span = math.gcd(sources, max(1, 256 // width))
    rows = span * width
    whole = pl.BlockSpec((sources, pieces, width, lanes), lambda i: (0, 0, 0, 0))
    part = pl.BlockSpec((span, width, lanes), lambda i: (i, 0, 0))
    return pl.pallas_call(
        functools.partial(kernel, lanes // head, own, head, 1.0 / math.sqrt(head), span),
        grid=(sources // span,),
        in_specs=[whole]
        + [part] * len(extra)
        + [
            pl.BlockSpec((rows, 1), lambda i: (i, 0)),
            pl.BlockSpec((rows, groups), lambda i: (i, 0)),
            pl.BlockSpec((1, length), lambda i: (0, 0)),
            pl.BlockSpec((groups, length), lambda i: (0, 0)),
        ],
        out_specs=[whole, pl.BlockSpec((8, lanes), lambda i: (0, 0))] if extra else part,
        out_shape=outs,
        scratch_shapes=scratch,
        compiler_params=pltpu.CompilerParams(vmem_limit_bytes=48 * 1024 * 1024),
    )(qkv, *extra, position[:, None], segments.T, position[None, :], segments)


def attend(qkv, position, segments, own, head):
    sources, _, width, lanes = qkv.shape
    outs = jax.ShapeDtypeStruct((sources, width, lanes), jnp.bfloat16)
    return attention_call(attend_kernel, (), outs, [], own, head, qkv, position, segments)


def attend_back(qkv, context, grad, position, segments, own, head):
    lanes = qkv.shape[-1]
    outs = [
        jax.ShapeDtypeStruct(qkv.shape, jnp.bfloat16),
        jax.ShapeDtypeStruct((8, lanes), jnp.float32),
    ]
    scratch = [pltpu.VMEM((lanes, position.shape[0]), jnp.float32)] * 2
    return attention_call(
        attend_back_kernel, (context, grad), outs, scratch, own, head, qkv, position, segments
    )


def body(
    n_ctx,
    n_fsdp,
    block_input,
    cotangent,
    block_table,
    segments,
    gain_one,
    shift_one,
    w_mix,
    bias_query,
    bias_value,
    w_merge,
    bias_merge,
    gain_two,
    shift_two,
    w_expand,
    bias_expand,
    w_reduce,
    bias_reduce,
):
    groups, width, model = block_input.shape
    length = segments.shape[1]
    heads = HEADS
    head = model // heads
    half_heads = heads // 2
    scale = 1.0 / math.sqrt(head)
    (
        gain_one,
        shift_one,
        w_mix,
        bias_query,
        bias_value,
        w_merge,
        bias_merge,
        gain_two,
        shift_two,
        w_expand,
        bias_expand,
        w_reduce,
        bias_reduce,
    ) = (
        lax.all_gather(gain_one, "fsdp", axis=0, tiled=True),
        lax.all_gather(shift_one, "fsdp", axis=0, tiled=True),
        lax.all_gather(w_mix, "fsdp", axis=0, tiled=True),
        lax.all_gather(bias_query, "fsdp", axis=0, tiled=True),
        lax.all_gather(bias_value, "fsdp", axis=0, tiled=True),
        lax.all_gather(w_merge, "fsdp", axis=0, tiled=True),
        lax.all_gather(bias_merge, "fsdp", axis=0, tiled=True),
        lax.all_gather(gain_two, "fsdp", axis=0, tiled=True),
        lax.all_gather(shift_two, "fsdp", axis=0, tiled=True),
        lax.all_gather(w_expand, "fsdp", axis=0, tiled=True),
        lax.all_gather(bias_expand, "fsdp", axis=0, tiled=True),
        lax.all_gather(w_reduce, "fsdp", axis=0, tiled=True),
        lax.all_gather(bias_reduce, "fsdp", axis=0, tiled=True),
    )
    key_position = slot_positions(block_table, width // 2)
    by_heads = heads % n_ctx == 0
    if not by_heads:
        first_slot = lax.axis_index("ctx") * width
        query_position = lax.dynamic_slice_in_dim(key_position, first_slot, width)
        query_segment = lax.dynamic_slice_in_dim(segments, first_slot, width, axis=1)
        visible = jnp.logical_and(
            key_position[None, None, :] <= query_position[None, :, None],
            segments[:, None, :] == query_segment[:, :, None],
        )
    tokens = block_input.reshape(groups * width, model).astype(jnp.float32)
    normed_one, inverse_one, first_in = norm_forward(tokens, gain_one, shift_one)
    offsets = jnp.concatenate([bias_query, jnp.zeros_like(bias_query), bias_value]).astype(
        jnp.float32
    )
    mixed = (jnp.dot(first_in, w_mix, preferred_element_type=jnp.float32) + offsets).astype(
        jnp.bfloat16
    )
    if by_heads:
        own = heads // n_ctx
        qkv = to_heads(mixed, groups, 3, n_ctx)
        context = attend(qkv, key_position, segments, own, head)
        context_rows = to_tokens(context[:, None], groups)
    else:
        queries = mixed[:, :model].reshape(groups, width, heads, head)
        local_pairs = mixed[:, model:].reshape(groups, width, 2 * model)
        pairs = lax.all_gather(local_pairs, "ctx", axis=1, tiled=True)
        keys = pairs[:, :, :model].reshape(groups, length, heads, head)
        values = pairs[:, :, model:].reshape(groups, length, heads, head)
        context_parts, log_parts = ([], [])
        for half in range(2):
            first = half * half_heads
            part_scores = (
                jnp.einsum(
                    "gshd,gthd->ghst",
                    queries[:, :, first : first + half_heads],
                    keys[:, :, first : first + half_heads],
                    preferred_element_type=jnp.float32,
                )
                * scale
            )
            expo = jnp.where(visible[:, None], jnp.exp(part_scores), 0.0)
            total = jnp.sum(expo, axis=-1)
            summed = jnp.einsum(
                "ghst,gthd->gshd",
                expo.astype(jnp.bfloat16),
                values[:, :, first : first + half_heads],
                preferred_element_type=jnp.float32,
            )
            context_parts.append(summed / jnp.swapaxes(total, 1, 2)[..., None])
            log_parts.append(jnp.log(total))
        context = jnp.concatenate(context_parts, axis=2).astype(jnp.bfloat16)
        log_total = jnp.concatenate(log_parts, axis=1)
        context_rows = context.reshape(groups * width, model)
    resid = (
        tokens
        + jnp.dot(context_rows, w_merge, preferred_element_type=jnp.float32)
        + bias_merge.astype(jnp.float32)
    )
    normed_two, inverse_two, second_in = norm_forward(resid, gain_two, shift_two)
    pre = jnp.dot(second_in, w_expand, preferred_element_type=jnp.float32) + bias_expand.astype(
        jnp.float32
    )
    act = gelu_value(pre).astype(jnp.bfloat16)
    block_output = (
        resid
        + jnp.dot(act, w_reduce, preferred_element_type=jnp.float32)
        + bias_reduce.astype(jnp.float32)
    ).astype(jnp.bfloat16)
    upstream = cotangent.reshape(groups * width, model)
    incoming = upstream.astype(jnp.float32)
    bits = list(range(halving_bits(n_ctx)))
    swapped = bits[1::-1] + bits[2:]
    reduce = weight_grad(act, upstream, bits, n_ctx, n_fsdp)
    gated = advance(upstream, reduce)
    grad_pre = jnp.einsum(
        "tj,ij->ti", gated, w_reduce, preferred_element_type=jnp.float32
    ) * gelu_slope(pre)
    pre_rounded = grad_pre.astype(jnp.bfloat16)
    expand = weight_grad(second_in, pre_rounded, swapped, n_ctx, n_fsdp)
    pre_rounded = advance(pre_rounded, expand)
    grad_second = jnp.einsum("tj,ij->ti", pre_rounded, w_expand, preferred_element_type=jnp.float32)
    grad_resid = incoming + norm_backward(grad_second, normed_two, inverse_two, gain_two)
    resid_rounded = grad_resid.astype(jnp.bfloat16)
    grad_context = jnp.einsum(
        "tj,ij->ti", resid_rounded, w_merge, preferred_element_type=jnp.float32
    ).astype(jnp.bfloat16)
    if by_heads:
        grad_heads = to_heads(grad_context, groups, 1, n_ctx)[:, 0]
        merge = weight_grad(context_rows, resid_rounded, bits, n_ctx, n_fsdp)
        grad_heads = advance(grad_heads, merge, reduce, expand)
        grad_qkv, sums = attend_back(
            qkv, context, grad_heads, key_position, segments, own, head
        )
        bias_sums = jnp.sum(sums[:2].reshape(2, groups, own * head), axis=1)
        placed = jnp.zeros((2, n_ctx, own * head), jnp.float32)
        placed = lax.dynamic_update_slice_in_dim(
            placed, bias_sums[:, None], lax.axis_index("ctx"), 1
        )
        query_sum, value_sum = placed.reshape(2, model)
        grad_mixed = advance(to_tokens(grad_qkv, groups), reduce, expand, merge)
    else:
        merge = weight_grad(context_rows, resid_rounded, bits, n_ctx, n_fsdp)
        delta = jnp.sum(
            (grad_context.astype(jnp.float32) * context_rows.astype(jnp.float32)).reshape(
                groups, width, heads, head
            ),
            axis=-1,
        )
        delta = jnp.swapaxes(delta, 1, 2)
        grad_heads = grad_context.reshape(groups, width, heads, head)
        query_parts, key_parts, value_parts = ([], [], [])
        for half in range(2):
            first = half * half_heads
            query_part = queries[:, :, first : first + half_heads]
            key_part = keys[:, :, first : first + half_heads]
            value_part = values[:, :, first : first + half_heads]
            grad_part = grad_heads[:, :, first : first + half_heads]
            part_scores = (
                jnp.einsum("gshd,gthd->ghst", query_part, key_part, preferred_element_type=jnp.float32)
                * scale
            )
            prob = jnp.where(
                visible[:, None],
                jnp.exp(part_scores - log_total[:, first : first + half_heads, :, None]),
                0.0,
            )
            dprob = jnp.einsum(
                "gshd,gthd->ghst", grad_part, value_part, preferred_element_type=jnp.float32
            )
            grad_score = prob * (dprob - delta[:, first : first + half_heads, :, None])
            score_rounded = grad_score.astype(jnp.bfloat16)
            query_parts.append(
                jnp.einsum(
                    "ghst,gthd->gshd", score_rounded, key_part, preferred_element_type=jnp.float32
                )
                * scale
            )
            key_term = (
                jnp.einsum(
                    "ghst,gshd->gthd", score_rounded, query_part, preferred_element_type=jnp.float32
                )
                * scale
            )
            value_term = jnp.einsum(
                "ghst,gshd->gthd",
                prob.astype(jnp.bfloat16),
                grad_part,
                preferred_element_type=jnp.float32,
            )
            key_sum, value_sum = (
                lax.psum_scatter(
                    key_term.reshape(groups, length, half_heads * head),
                    "ctx",
                    scatter_dimension=1,
                    tiled=True,
                ),
                lax.psum_scatter(
                    value_term.reshape(groups, length, half_heads * head),
                    "ctx",
                    scatter_dimension=1,
                    tiled=True,
                ),
            )
            key_parts.append(key_sum)
            value_parts.append(value_sum)
        grad_query = jnp.concatenate(query_parts, axis=2)
        grad_key = jnp.concatenate(key_parts, axis=2)
        grad_value = jnp.concatenate(value_parts, axis=2)
        query_rows_grad = grad_query.reshape(groups * width, model)
        key_rows_grad = grad_key.reshape(groups * width, model)
        value_rows_grad = grad_value.reshape(groups * width, model)
        query_sum = jnp.sum(query_rows_grad, axis=0)
        value_sum = jnp.sum(value_rows_grad, axis=0)
        grad_mixed = jnp.concatenate(
            [query_rows_grad, key_rows_grad, value_rows_grad], axis=1
        ).astype(jnp.bfloat16)
    middle = grad_mixed.shape[1] // 2
    mix_low = weight_grad(first_in, grad_mixed[:, :middle], bits, n_ctx, n_fsdp)
    mix_high = weight_grad(first_in, grad_mixed[:, middle:], swapped, n_ctx, n_fsdp)
    grad_mixed = advance(grad_mixed, mix_low, mix_high)
    grad_first = jnp.einsum("tj,ij->ti", grad_mixed, w_mix, preferred_element_type=jnp.float32)
    grad_tokens = grad_resid + norm_backward(grad_first, normed_one, inverse_one, gain_one)
    vectors = vector_grads(
        [
            jnp.sum(grad_first * normed_one, axis=0),
            jnp.sum(grad_first, axis=0),
            query_sum,
            value_sum,
            jnp.sum(grad_resid, axis=0),
            jnp.sum(grad_second * normed_two, axis=0),
            jnp.sum(grad_second, axis=0),
            jnp.sum(grad_pre, axis=0),
            jnp.sum(incoming, axis=0),
        ],
        bits,
        n_ctx,
        n_fsdp,
    )
    grad_tokens = advance(grad_tokens, vectors, mix_low, mix_high, reduce, expand, merge)
    for _ in bits:
        grad_tokens = advance(grad_tokens, vectors, mix_low, mix_high, reduce, expand, merge)
    own = vectors.finish().reshape(-1)
    sums, at = [], 0
    for piece in (model,) * 7 + (pre.shape[1], model):
        sums.append(own[at : at + piece // (n_ctx * n_fsdp)])
        at += piece // (n_ctx * n_fsdp)
    return (
        block_output.reshape(groups, width, model),
        grad_tokens.reshape(groups, width, model),
        sums[0],
        sums[1],
        jnp.concatenate([mix_low.finish(), mix_high.finish()], axis=1),
        sums[2],
        sums[3],
        merge.finish(),
        sums[4],
        sums[5],
        sums[6],
        expand.finish(),
        sums[7],
        reduce.finish(),
        sums[8],
    )


def solution(mesh):
    in_specs = (
        P("fsdp", "ctx", None),
        P("fsdp", "ctx", None),
        P(),
        P("fsdp", None),
        P("fsdp"),
        P("fsdp"),
        P("fsdp", None),
        P("fsdp"),
        P("fsdp"),
        P("fsdp", None),
        P("fsdp"),
        P("fsdp"),
        P("fsdp"),
        P("fsdp", None),
        P("fsdp"),
        P("fsdp", None),
        P("fsdp"),
    )
    out_specs = (
        P("fsdp", "ctx", None),
        P("fsdp", "ctx", None),
        P(("ctx", "fsdp")),
        P(("ctx", "fsdp")),
        P(("ctx", "fsdp"), None),
        P(("ctx", "fsdp")),
        P(("ctx", "fsdp")),
        P(("ctx", "fsdp"), None),
        P(("ctx", "fsdp")),
        P(("ctx", "fsdp")),
        P(("ctx", "fsdp")),
        P(("ctx", "fsdp"), None),
        P(("ctx", "fsdp")),
        P(("ctx", "fsdp"), None),
        P(("ctx", "fsdp")),
    )
    return jax.shard_map(
        functools.partial(body, mesh.shape["ctx"], mesh.shape["fsdp"]),
        mesh=mesh,
        in_specs=in_specs, out_specs=out_specs, check_vma=False)
```
